32 devices in a mesh: dp: 4 (over y, core), seq: 8 (over z, x).
Axes of the slice: x: 2, y: 2, z: 4, core: 2. Of those that a mesh axis runs over, the one named last changes fastest.
Arguments:
- qkv_teacher: bfloat16 [4, 3, 16, 64, 768], P('dp', None, None, 'seq'), may hold values from -5.2 to 5.2, as said below
- qkv_student: bfloat16 [4, 3, 16, 64, 768], P('dp', None, None, 'seq'), may hold values from -5.2 to 5.2, as said below
- proto_teacher: bfloat16 [768, 8192], P(None, 'seq'), may hold values from -0.21875 to 0.21875
- proto_student: bfloat16 [768, 8192], P(None, 'seq'), may hold values from -2.25 to 2.25
- center: float32 [8192], P('seq'), may hold values from -9 to 1
- pairing: int32 [4], replicated, may hold values from 0 to 3, as said below
Outputs:
- teacher_out: bfloat16 [4, 16, 64, 768], P('dp', None, 'seq')
- student_out: bfloat16 [4, 16, 64, 768], P('dp', None, 'seq')
- loss: float32 [4], P('dp')
The draws below stay inside these ranges and needn't reach their ends.
Inputs may be any that keep to these rules, and one draw needn't show every extreme that they name: `qkv_teacher`: random normal values; some positions of the keys may repeat a query's pattern. `qkv_student`: random normal values; some positions of the keys may repeat a query's pattern. pairing[pairing[v]] == v and pairing[v] != v for every view v.
All inputs are finite; a program needn't handle non-finite values.
Results may differ from the reference program's by a relative error of at most 0.001.
The reference program's roundings to bfloat16 on the way count: a program that leaves them out, or rounds other values in their place, can miss the bound.
Values may be sent and summed in bfloat16 or wider, within the bound.
No kernel may reach another device: no remote copies, remote signals or barrier semaphores. Data moves between devices by JAX's collectives and lax.ppermute only.
A program may use at most 64 MiB of HBM per device.

```python
import jax
import jax.numpy as jnp
from jax import lax

HEADS = 12
HD = 64
F = 16
K = 8192
DA = 768
P_SIZE = 64
VIEWS = 4


def qkv_field(key):
    values = jnp.clip(jax.random.normal(key, (VIEWS, 3, F, P_SIZE, DA), jnp.float32), -5.0, 5.0)
    return values.astype(jnp.bfloat16)


def draw_qkv_teacher(key, part):
    return qkv_field(jax.random.fold_in(key, 11))


def draw_qkv_student(key, part):
    return qkv_field(jax.random.fold_in(key, 23))


def draw_proto_student(key, part):
    values = jnp.clip(jax.random.normal(key, (DA, K), jnp.float32), -5.0, 5.0) * DA ** (-0.5)
    values = jnp.clip(values, -2.2, 2.2)
    return values.astype(jnp.bfloat16)


def draw_center(key, part):
    values = jnp.clip(0.3 * jax.random.normal(key, (K,), jnp.float32), -1.0, 1.0)
    return values


def draw_pairing(key, part):
    order = jax.random.permutation(key, VIEWS).astype(jnp.int32)
    swapped = order.reshape(-1, 2)[:, ::-1].reshape(-1)
    return jnp.zeros((VIEWS,), jnp.int32).at[order].set(swapped)


def steps_of(stream_key, shape, shards, low, largest):
    loudness = 1.0
    for dim, parts in shards:
        heights = jax.random.uniform(jax.random.fold_in(jax.random.fold_in(stream_key, 6), dim), (parts,), jnp.float32, low / len(shards), largest / len(shards))
        loudness = loudness * jnp.repeat(jnp.exp(heights), shape[dim] // parts).reshape((-1,) + (1,) * (len(shape) - 1 - dim))
    return loudness


def scatter_about(own_key, extent, deviation, bound, cuts=(), held_as=jnp.bfloat16):
    level = steps_of(own_key, extent, cuts, -0.22, 0.18) if cuts else 1.0
    result = jax.random.normal(own_key, extent, jnp.float32) * deviation * level
    return jnp.minimum(jnp.maximum(result, -bound), bound).astype(held_as)


def setup_inputs(seed: int = 0) -> dict:
    splits = jax.random.split(jax.random.key(seed), 7)
    return {
        "qkv_teacher": draw_qkv_teacher(jax.random.fold_in(splits[6], 71), 0),
        "qkv_student": draw_qkv_student(jax.random.fold_in(splits[6], 71), 0),
        "proto_teacher": scatter_about(splits[2], (DA, K), DA ** -0.5, 0.21875, ((1, 8),)),
        "proto_student": draw_proto_student(jax.random.fold_in(splits[6], 71), 0),
        "center": draw_center(jax.random.fold_in(splits[6], 71), 0),
        "pairing": draw_pairing(jax.random.fold_in(splits[6], 71), 0),
    }


tau_teacher = 0.07
tau_student = 0.1
norm_eps = 1e-06

def attend_item(item):
    scores = lax.dot_general(item[0], item[1], (((1,), (1,)), ((), ())), preferred_element_type=jnp.float32) * HD ** (-0.5)
    weights = jax.nn.softmax(scores, axis=-1).astype(jnp.bfloat16)
    return jnp.dot(weights, item[2], preferred_element_type=jnp.float32).astype(jnp.bfloat16)

def view_attention(single_view):
    items = single_view.reshape(3, F, P_SIZE, HEADS, HD).transpose(1, 3, 0, 2, 4).reshape(F * HEADS, 3, P_SIZE, HD)
    outputs = lax.map(attend_item, items)
    return outputs.reshape(F, HEADS, P_SIZE, HD).transpose(0, 2, 1, 3).reshape(F, P_SIZE, HEADS * HD)

def unit_rows(values):
    return values * lax.rsqrt(lax.optimization_barrier(jnp.mean(values * values, axis=-1, keepdims=True)) + norm_eps)

def reference(qkv_teacher, qkv_student, proto_teacher, proto_student, center, pairing):
    teacher_out = lax.map(view_attention, qkv_teacher)
    student_out = lax.map(view_attention, qkv_student)
    scale = 1.0 / (F * P_SIZE)
    pooled_teacher = lax.optimization_barrier(jnp.sum(teacher_out.astype(jnp.float32), axis=(1, 2))) * scale
    pooled_student = lax.optimization_barrier(jnp.sum(student_out.astype(jnp.float32), axis=(1, 2))) * scale
    logit_teacher = jnp.dot(unit_rows(pooled_teacher), proto_teacher.astype(jnp.float32), precision=lax.Precision.HIGHEST)
    logit_student = jnp.dot(unit_rows(pooled_student), proto_student.astype(jnp.float32), precision=lax.Precision.HIGHEST)
    sharp = (logit_teacher - center[None, :]) / tau_teacher
    soft = logit_student / tau_student
    partner = sharp[pairing]
    probs = jax.nn.softmax(partner, axis=-1)
    loss = jax.nn.logsumexp(soft, axis=-1) - lax.optimization_barrier(jnp.sum(probs * soft, axis=-1))
    return (teacher_out, student_out, loss)
```

```python
import functools

import jax
import jax.numpy as jnp
from jax import lax
from jax.experimental import pallas as pl
from jax.experimental.pallas import tpu as pltpu
from jax.sharding import PartitionSpec as P

HD = 64
PAIR = 2 * HD

tau_teacher = 0.07
tau_student = 0.1
norm_eps = 1e-06


def attend_frame_pair(q, k, v, low):
    zero = jnp.zeros_like(k)
    keys = jnp.concatenate([jnp.where(low, k, zero), jnp.where(low, zero, k)], axis=0)
    values = jnp.concatenate([jnp.where(low, v, zero), jnp.where(low, zero, v)], axis=0)
    tokens = q.shape[0]
    scores = (
        lax.dot_general(
            q.astype(jnp.bfloat16),
            keys.astype(jnp.bfloat16),
            (((1,), (1,)), ((), ())),
            preferred_element_type=jnp.float32,
        )
        * HD ** (-0.5)
    )
    first = lax.broadcasted_iota(jnp.int32, scores.shape, 1) < tokens
    least = jnp.full_like(scores, -jnp.inf)
    top = jnp.where(
        first,
        jnp.max(jnp.where(first, scores, least), axis=-1, keepdims=True),
        jnp.max(jnp.where(first, least, scores), axis=-1, keepdims=True),
    )
    raised = jnp.exp(scores - top)
    none = jnp.zeros_like(raised)
    total = jnp.where(
        first,
        jnp.sum(jnp.where(first, raised, none), axis=-1, keepdims=True),
        jnp.sum(jnp.where(first, none, raised), axis=-1, keepdims=True),
    )
    weights = (raised / total).astype(jnp.bfloat16)
    return jnp.dot(
        weights, values.astype(jnp.bfloat16), preferred_element_type=jnp.float32
    ).astype(jnp.bfloat16)


def attend_blocks(me, blocks, out_ref):
    _, frames, pos_dev, width = blocks[0].shape
    low = lax.broadcasted_iota(jnp.int32, (1, PAIR), 1) < HD
    sums = []
    for pair in range(width // PAIR):
        lanes = pl.ds(pair * PAIR, PAIR)
        total = None
        for frame in range(frames):
            q, k, v = (
                jnp.concatenate(
                    [blk[part, frame, :, lanes].astype(jnp.float32) for blk in blocks], axis=0
                )
                for part in range(3)
            )
            out = attend_frame_pair(q, k, v, low).astype(jnp.float32)
            for b in range(len(blocks)):
                piece = out[b * pos_dev : (b + 1) * pos_dev]
                out_ref[me ^ b, frame, :, lanes] = piece.astype(jnp.bfloat16)
            part = jnp.sum(out, axis=0, keepdims=True)
            total = part if total is None else total + part
        sums.append(total)
    return jnp.concatenate(sums, axis=1)


def teacher_kernel(nseq, me_ref, *refs):
    blocks, (out_ref, pool_ref) = refs[:nseq], refs[nseq:]
    pool_ref[...] = attend_blocks(me_ref[0], blocks, out_ref)


def student_kernel(nseq, me_ref, *refs):
    blocks, rows_ref, (out_ref, pool_ref) = refs[:nseq], refs[nseq], refs[nseq + 1 :]
    own = attend_blocks(me_ref[0], blocks, out_ref)
    teacher = rows_ref[me_ref[1]]
    for d in range(nseq):
        pool_ref[d, 0:1, :] = teacher
        pool_ref[d, 1:2, :] = own


def unit_vector(values):
    return values * lax.rsqrt(jnp.mean(values * values, axis=-1, keepdims=True) + norm_eps)


def full_product(row, proto):
    high = row.astype(jnp.bfloat16).astype(jnp.float32)
    rest = row - high
    mid = rest.astype(jnp.bfloat16).astype(jnp.float32)
    last = rest - mid
    index = lax.broadcasted_iota(jnp.int32, (16, row.shape[1]), 0)
    terms = jnp.where(
        index == 0, high, jnp.where(index == 1, mid, jnp.where(index == 2, last, 0.0))
    )
    out = jnp.dot(terms.astype(jnp.bfloat16), proto, preferred_element_type=jnp.float32)
    return out[2:3] + out[1:2] + out[0:1]


def logit_kernel(scale, pools_ref, proto_t_ref, proto_s_ref, center_ref, stats_ref):
    pooled = jnp.sum(pools_ref[...], axis=0) * scale
    logit_t = full_product(unit_vector(pooled[0:1]), proto_t_ref[...])
    logit_s = full_product(unit_vector(pooled[1:2]), proto_s_ref[...])
    sharp = (logit_t - center_ref[...]) / tau_teacher
    soft = logit_s / tau_student
    top_t = jnp.max(sharp, axis=-1, keepdims=True)
    raised = jnp.exp(sharp - top_t)
    top_s = jnp.max(soft, axis=-1, keepdims=True)
    parts = (
        top_t,
        jnp.sum(raised, axis=-1, keepdims=True),
        jnp.sum(raised * soft, axis=-1, keepdims=True),
        top_s,
        jnp.sum(jnp.exp(soft - top_s), axis=-1, keepdims=True),
    )
    index = lax.broadcasted_iota(jnp.int32, (8, 128), 0)
    block = jnp.zeros((8, 128), jnp.float32)
    for i, part in enumerate(parts):
        block = jnp.where(index == i, part, block)
    for d in range(stats_ref.shape[0]):
        stats_ref[d] = block


def merge_partials(stats):
    top_t = jnp.max(stats[:, 0:1, :], axis=0)
    share_t = jnp.exp(stats[:, 0:1, :] - top_t)
    top_s = jnp.max(stats[:, 3:4, :], axis=0)
    share_s = jnp.exp(stats[:, 3:4, :] - top_s)
    total_t = jnp.sum(stats[:, 1:2, :] * share_t, axis=0)
    cross = jnp.sum(stats[:, 2:3, :] * share_t, axis=0)
    total_s = jnp.sum(stats[:, 4:5, :] * share_s, axis=0)
    return top_s + jnp.log(total_s) - cross / total_t


def loss_kernel(stats_ref, loss_ref):
    loss_ref[0] = merge_partials(stats_ref[...])[0, 0]


VMEM = pl.BlockSpec(memory_space=pltpu.VMEM)
SMEM = pl.BlockSpec(memory_space=pltpu.SMEM)


def logits_and_loss(pools, proto_teacher, proto_student, center, scale):
    nseq = pools.shape[0]
    stats = pl.pallas_call(
        functools.partial(logit_kernel, scale),
        out_shape=jax.ShapeDtypeStruct((nseq, 8, 128), jnp.float32),
        in_specs=[VMEM] * 4,
        out_specs=VMEM,
        name="logits",
    )(pools, proto_teacher, proto_student, center.reshape(1, -1))
    stats = lax.all_to_all(stats, "seq", 0, 0, tiled=True)
    return pl.pallas_call(
        loss_kernel,
        out_shape=jax.ShapeDtypeStruct((1,), jnp.float32),
        in_specs=[VMEM],
        out_specs=SMEM,
        name="loss",
    )(stats)


def exchange(qkv, me, nseq):
    frames, pos_dev, width = qkv.shape[2:]
    per_dev = frames // nseq
    split = qkv[0].reshape(3, nseq, per_dev, pos_dev, width)
    blocks = [lax.dynamic_index_in_dim(split, me ^ b, 1, keepdims=False) for b in range(nseq)]
    order = sorted(range(1, nseq), reverse=True)
    arrived = {
        b: lax.ppermute(blocks[b], "seq", [(i, i ^ b) for i in range(nseq)]) for b in order
    }
    return [blocks[0]] + [arrived[b] for b in range(1, nseq)]


def by_frames(qkv_teacher, qkv_student, proto_teacher, proto_student, center, pairing):
    nseq = lax.axis_size("seq")
    frames, pos_dev, width = qkv_teacher.shape[2:]
    per_dev = frames // nseq
    me = lax.axis_index("seq")
    own_view = lax.axis_index("dp")
    partner = jnp.sum(jnp.where(jnp.arange(pairing.shape[0]) == own_view, pairing, 0))
    where = jnp.stack([me, partner]).astype(jnp.int32)
    blocks_t = exchange(qkv_teacher, me, nseq)
    blocks_s = exchange(qkv_student, me, nseq)
    sent = jax.ShapeDtypeStruct((nseq, per_dev, pos_dev, width), jnp.bfloat16)
    out_t, pool_t = pl.pallas_call(
        functools.partial(teacher_kernel, nseq),
        out_shape=(sent, jax.ShapeDtypeStruct((1, width), jnp.float32)),
        in_specs=[SMEM] + [VMEM] * nseq,
        out_specs=(VMEM, VMEM),
        name="teacher",
    )(where, *blocks_t)
    rows = lax.all_gather(pool_t, "dp")
    out_s, pools = pl.pallas_call(
        functools.partial(student_kernel, nseq),
        out_shape=(sent, jax.ShapeDtypeStruct((nseq, 2, width), jnp.float32)),
        in_specs=[SMEM] + [VMEM] * (nseq + 1),
        out_specs=(VMEM, VMEM),
        name="student",
    )(where, *blocks_s, rows)
    pools = lax.all_to_all(pools, "seq", 0, 0, tiled=True)
    scale = 1.0 / (frames * pos_dev * nseq)
    loss = logits_and_loss(pools, proto_teacher, proto_student, center, scale)
    teacher_out = lax.all_to_all(out_t, "seq", 0, 0, tiled=True)
    student_out = lax.all_to_all(out_s, "seq", 0, 0, tiled=True)
    shape = (1, frames, pos_dev, width)
    return teacher_out.reshape(shape), student_out.reshape(shape), loss


def attend_items(items):
    q, k, v = items[:, 0], items[:, 1], items[:, 2]
    scores = jnp.einsum("iqd,ikd->iqk", q, k, preferred_element_type=jnp.float32) * HD ** (-0.5)
    raised = jnp.exp(scores - jnp.max(scores, axis=-1, keepdims=True))
    weights = (raised / jnp.sum(raised, axis=-1, keepdims=True)).astype(jnp.bfloat16)
    out = jnp.einsum("iqk,ikd->iqd", weights, v, preferred_element_type=jnp.float32)
    return out.astype(jnp.bfloat16)


def attend_spread(qkv, nseq):
    frames, pos_dev, width = qkv.shape[2:]
    heads = width // HD
    per_dev = frames * heads // nseq
    items = qkv[0].reshape(3, frames, pos_dev, heads, HD).transpose(1, 3, 0, 2, 4)
    items = items.reshape(nseq, per_dev, 3, pos_dev * HD)
    items = lax.all_to_all(items, "seq", split_axis=0, concat_axis=3, tiled=True)
    out = attend_items(items.reshape(per_dev, 3, nseq * pos_dev, HD))
    out = out.reshape(1, per_dev, nseq, pos_dev * HD)
    out = lax.all_to_all(out, "seq", split_axis=2, concat_axis=0, tiled=True)
    out = out.reshape(frames, heads, pos_dev, HD).transpose(0, 2, 1, 3)
    out = out.reshape(1, frames, pos_dev, width)
    return out, jnp.sum(out[0].astype(jnp.float32), axis=(0, 1))


def by_items(qkv_teacher, qkv_student, proto_teacher, proto_student, center, pairing):
    nseq = lax.axis_size("seq")
    frames, pos_dev, width = qkv_teacher.shape[2:]
    own_view = lax.axis_index("dp")
    partner = jnp.sum(jnp.where(jnp.arange(pairing.shape[0]) == own_view, pairing, 0))
    teacher_out, pool_t = attend_spread(qkv_teacher, nseq)
    student_out, pool_s = attend_spread(qkv_student, nseq)
    rows = lax.all_gather(pool_t, "dp")
    pool_t = lax.dynamic_index_in_dim(rows, partner, 0, keepdims=False)
    pools = jnp.broadcast_to(jnp.stack([pool_t, pool_s]), (nseq, 2, width))
    pools = lax.all_to_all(pools, "seq", 0, 0, tiled=True)
    scale = 1.0 / (frames * pos_dev * nseq)
    loss = logits_and_loss(pools, proto_teacher, proto_student, center, scale)
    return teacher_out, student_out, loss


def local(qkv_teacher, *rest):
    nseq = lax.axis_size("seq")
    frames, pos_dev, width = qkv_teacher.shape[2:]
    whole_frames = (
        frames % nseq == 0
        and nseq & (nseq - 1) == 0
        and pos_dev % 8 == 0
        and width % PAIR == 0
        and pos_dev * nseq <= 64
    )
    return (by_frames if whole_frames else by_items)(qkv_teacher, *rest)


def solution(mesh):
    placed = (
        P("dp", None, None, "seq", None),
        P("dp", None, None, "seq", None),
        P(None, "seq"),
        P(None, "seq"),
        P("seq"),
        P(),
    )
    return jax.shard_map(
        local,
        mesh=mesh,
        in_specs=placed,
        out_specs=(P("dp", None, "seq", None), P("dp", None, "seq", None), P("dp")),
        check_vma=False,
    )
```

```python
import functools

import jax
import jax.numpy as jnp
from jax import lax
from jax.experimental import pallas as pl
from jax.experimental.pallas import tpu as pltpu
from jax.sharding import PartitionSpec as P


HD = 64
PAIR = 2 * HD

tau_teacher = 0.07
tau_student = 0.1
norm_eps = 1e-06


def gathered(blocks, part, frame, lanes):
    return jnp.concatenate(
        [blk[part, frame, :, lanes].astype(jnp.float32) for blk in blocks], axis=0
    )


def attend_blocks(me, blocks, out_ref):
    _, frames, pos_dev, width = blocks[0].shape
    tokens = pos_dev * len(blocks)
    low = lax.broadcasted_iota(jnp.int32, (1, PAIR), 1) < HD
    sums = []
    for pair in range(width // PAIR):
        lanes = pl.ds(pair * PAIR, PAIR)
        weights = []
        for frame in range(frames):
            q = gathered(blocks, 0, frame, lanes)
            k = gathered(blocks, 1, frame, lanes).astype(jnp.bfloat16)
            zero = jnp.zeros_like(q)
            queries = jnp.concatenate([jnp.where(low, q, zero), jnp.where(low, zero, q)], axis=0)
            scores = (
                lax.dot_general(
                    k,
                    queries.astype(jnp.bfloat16),
                    (((1,), (1,)), ((), ())),
                    preferred_element_type=jnp.float32,
                )
                * HD ** (-0.5)
            )
            raised = jnp.exp(scores - jnp.max(scores, axis=0, keepdims=True))
            share = 1.0 / jnp.sum(raised, axis=0, keepdims=True)
            weights.append((raised * share).astype(jnp.bfloat16))
        total = None
        for frame in range(frames):
            v = gathered(blocks, 2, frame, lanes).astype(jnp.bfloat16)
            both = lax.dot_general(
                weights[frame], v, (((0,), (0,)), ((), ())), preferred_element_type=jnp.float32
            )
            out = jnp.where(low, both[:tokens], both[tokens:])
            out = out.astype(jnp.bfloat16).astype(jnp.float32)
            for b in range(len(blocks)):
                piece = out[b * pos_dev : (b + 1) * pos_dev]
                out_ref[me ^ b, frame, :, lanes] = piece.astype(jnp.bfloat16)
            part = jnp.sum(out, axis=0, keepdims=True)
            total = part if total is None else total + part
        sums.append(total)
    return jnp.concatenate(sums, axis=1)


def teacher_kernel(nseq, *refs):
    blocks, (out_ref, pool_ref) = refs[:nseq], refs[nseq:]
    pool_ref[...] = attend_blocks(lax.axis_index("seq"), blocks, out_ref)


def student_kernel(nseq, *refs):
    blocks, teacher_ref, (out_ref, pool_ref) = refs[:nseq], refs[nseq], refs[nseq + 1 :]
    own = attend_blocks(lax.axis_index("seq"), blocks, out_ref)
    both = jnp.concatenate([teacher_ref[...], own], axis=0)
    for d in range(pool_ref.shape[0]):
        pool_ref[d] = both


def unit_vector(values):
    return values * lax.rsqrt(jnp.mean(values * values, axis=-1, keepdims=True) + norm_eps)


def full_product(row, proto):
    high = row.astype(jnp.bfloat16).astype(jnp.float32)
    rest = row - high
    mid = rest.astype(jnp.bfloat16).astype(jnp.float32)
    last = rest - mid
    index = lax.broadcasted_iota(jnp.int32, (16, row.shape[1]), 0)
    terms = jnp.where(
        index == 0, high, jnp.where(index == 1, mid, jnp.where(index == 2, last, 0.0))
    )
    out = jnp.dot(terms.astype(jnp.bfloat16), proto, preferred_element_type=jnp.float32)
    return out[2:3] + out[1:2] + out[0:1]


def logit_kernel(
    scale, pairing_ref, pools_ref, proto_t_ref, proto_s_ref, center_ref, stats_ref
):
    view = lax.axis_index("dp")
    teacher = jnp.sum(pools_ref[pairing_ref[view]], axis=0) * scale
    student = jnp.sum(pools_ref[view], axis=0) * scale
    logit_t = full_product(unit_vector(teacher[0:1]), proto_t_ref[...])
    logit_s = full_product(unit_vector(student[1:2]), proto_s_ref[...])
    sharp = (logit_t - center_ref[...]) / tau_teacher
    soft = logit_s / tau_student
    top_t = jnp.max(sharp, axis=-1, keepdims=True)
    raised = jnp.exp(sharp - top_t)
    top_s = jnp.max(soft, axis=-1, keepdims=True)
    parts = (
        top_t,
        jnp.sum(raised, axis=-1, keepdims=True),
        jnp.sum(raised * soft, axis=-1, keepdims=True),
        top_s,
        jnp.sum(jnp.exp(soft - top_s), axis=-1, keepdims=True),
    )
    index = lax.broadcasted_iota(jnp.int32, (8, 128), 0)
    block = jnp.zeros((8, 128), jnp.float32)
    for i, part in enumerate(parts):
        block = jnp.where(index == i, part, block)
    for d in range(stats_ref.shape[0]):
        stats_ref[d] = block


def merge_partials(stats):
    top_t = jnp.max(stats[:, 0:1, :], axis=0)
    share_t = jnp.exp(stats[:, 0:1, :] - top_t)
    top_s = jnp.max(stats[:, 3:4, :], axis=0)
    share_s = jnp.exp(stats[:, 3:4, :] - top_s)
    total_t = jnp.sum(stats[:, 1:2, :] * share_t, axis=0)
    cross = jnp.sum(stats[:, 2:3, :] * share_t, axis=0)
    total_s = jnp.sum(stats[:, 4:5, :] * share_s, axis=0)
    return top_s + jnp.log(total_s) - cross / total_t


def loss_kernel(stats_ref, loss_ref):
    loss_ref[0] = merge_partials(stats_ref[...])[0, 0]


VMEM = pl.BlockSpec(memory_space=pltpu.VMEM)
SMEM = pl.BlockSpec(memory_space=pltpu.SMEM)


def logits_and_loss(pairing, pools, proto_teacher, proto_student, center, scale):
    nseq = lax.axis_size("seq")
    stats = pl.pallas_call(
        functools.partial(logit_kernel, scale),
        out_shape=jax.ShapeDtypeStruct((nseq, 8, 128), jnp.float32),
        in_specs=[SMEM] + [VMEM] * 4,
        out_specs=VMEM,
        name="logits",
    )(pairing, pools, proto_teacher, proto_student, center.reshape(1, -1))
    stats = lax.all_to_all(stats, "seq", 0, 0, tiled=True)
    return pl.pallas_call(
        loss_kernel,
        out_shape=jax.ShapeDtypeStruct((1,), jnp.float32),
        in_specs=[VMEM],
        out_specs=SMEM,
        name="loss",
    )(stats)


def exchange(qkv, me, nseq):
    frames, pos_dev, width = qkv.shape[2:]
    per_dev = frames // nseq
    split = qkv[0].reshape(3, nseq, per_dev, pos_dev, width)
    blocks = [lax.dynamic_index_in_dim(split, me ^ b, 1, keepdims=False) for b in range(nseq)]
    order = sorted(range(1, nseq), reverse=True)
    arrived = {}
    for b in order:
        arrived[b] = lax.ppermute(blocks[b], "seq", [(i, i ^ b) for i in range(nseq)])
    return [blocks[0]] + [arrived[b] for b in range(1, nseq)]


def by_frames(qkv_teacher, qkv_student, proto_teacher, proto_student, center, pairing):
    views, nseq = lax.axis_size("dp"), lax.axis_size("seq")
    frames, pos_dev, width = qkv_teacher.shape[2:]
    per_dev = frames // nseq
    me = lax.axis_index("seq")
    blocks_t = exchange(qkv_teacher, me, nseq)
    blocks_s = exchange(qkv_student, me, nseq)
    sent = jax.ShapeDtypeStruct((nseq, per_dev, pos_dev, width), jnp.bfloat16)
    out_t, pool_t = pl.pallas_call(
        functools.partial(teacher_kernel, nseq),
        out_shape=(sent, jax.ShapeDtypeStruct((1, width), jnp.float32)),
        in_specs=[VMEM] * nseq,
        out_specs=(VMEM, VMEM),
        name="teacher",
    )(*blocks_t)
    out_s, pools = pl.pallas_call(
        functools.partial(student_kernel, nseq),
        out_shape=(sent, jax.ShapeDtypeStruct((views * nseq, 2, width), jnp.float32)),
        in_specs=[VMEM] * (nseq + 1),
        out_specs=(VMEM, VMEM),
        name="student",
    )(*blocks_s, pool_t)
    pools = lax.all_to_all(pools, ("dp", "seq"), 0, 0, tiled=True)
    pools = pools.reshape(views, nseq, 2, width)
    scale = 1.0 / (frames * pos_dev * nseq)
    loss = logits_and_loss(pairing, pools, proto_teacher, proto_student, center, scale)
    teacher_out = lax.all_to_all(out_t, "seq", 0, 0, tiled=True)
    student_out = lax.all_to_all(out_s, "seq", 0, 0, tiled=True)
    shape = (1, frames, pos_dev, width)
    return teacher_out.reshape(shape), student_out.reshape(shape), loss


def attend_items(items):
    q, k, v = items[:, 0], items[:, 1], items[:, 2]
    scores = jnp.einsum("iqd,ikd->iqk", q, k, preferred_element_type=jnp.float32) * HD ** (-0.5)
    raised = jnp.exp(scores - jnp.max(scores, axis=-1, keepdims=True))
    weights = (raised / jnp.sum(raised, axis=-1, keepdims=True)).astype(jnp.bfloat16)
    out = jnp.einsum("iqk,ikd->iqd", weights, v, preferred_element_type=jnp.float32)
    return out.astype(jnp.bfloat16)


def attend_spread(qkv, nseq):
    frames, pos_dev, width = qkv.shape[2:]
    heads = width // HD
    per_dev = frames * heads // nseq
    items = qkv[0].reshape(3, frames, pos_dev, heads, HD).transpose(1, 3, 0, 2, 4)
    items = items.reshape(nseq, per_dev, 3, pos_dev * HD)
    items = lax.all_to_all(items, "seq", split_axis=0, concat_axis=3, tiled=True)
    out = attend_items(items.reshape(per_dev, 3, nseq * pos_dev, HD))
    out = out.reshape(1, per_dev, nseq, pos_dev * HD)
    out = lax.all_to_all(out, "seq", split_axis=2, concat_axis=0, tiled=True)
    out = out.reshape(frames, heads, pos_dev, HD).transpose(0, 2, 1, 3)
    out = out.reshape(1, frames, pos_dev, width)
    return out, jnp.sum(out[0].astype(jnp.float32), axis=(0, 1))


def by_items(qkv_teacher, qkv_student, proto_teacher, proto_student, center, pairing):
    views, nseq = lax.axis_size("dp"), lax.axis_size("seq")
    frames, pos_dev, width = qkv_teacher.shape[2:]
    teacher_out, pool_t = attend_spread(qkv_teacher, nseq)
    student_out, pool_s = attend_spread(qkv_student, nseq)
    pools = jnp.broadcast_to(jnp.stack([pool_t, pool_s]), (nseq, 2, width))
    pools = jnp.sum(lax.all_to_all(pools, "seq", 0, 0, tiled=True), axis=0)
    pools = lax.all_gather(pools, "dp").reshape(views, 1, 2, width)
    scale = 1.0 / (frames * pos_dev * nseq)
    loss = logits_and_loss(pairing, pools, proto_teacher, proto_student, center, scale)
    return teacher_out, student_out, loss


def local(qkv_teacher, *rest):
    nseq = lax.axis_size("seq")
    frames, pos_dev, width = qkv_teacher.shape[2:]
    whole_frames = (
        frames % nseq == 0
        and nseq & (nseq - 1) == 0
        and pos_dev % 8 == 0
        and width % PAIR == 0
        and pos_dev * nseq <= 64
    )
    return (by_frames if whole_frames else by_items)(qkv_teacher, *rest)


def solution(mesh):
    placed = (
        P("dp", None, None, "seq", None),
        P("dp", None, None, "seq", None),
        P(None, "seq"),
        P(None, "seq"),
        P("seq"),
        P(),
    )
    return jax.shard_map(
        local,
        mesh=mesh,
        in_specs=placed,
        out_specs=(P("dp", None, "seq", None), P("dp", None, "seq", None), P("dp")),
        check_vma=False,
    )
```
